256 devices in a mesh: space: 64 (over y, z, core), chan: 4 (over x).
Axes of the slice: x: 4, y: 4, z: 8, core: 2. Of those that a mesh axis runs over, the one named last changes fastest.
Arguments:
- volume: bfloat16 [16, 256, 128, 128], P(None, 'space', 'chan'), may hold values from -6 to 6
- kernel: bfloat16 [27, 128, 128], P(None, None, 'chan'), may hold values from -0.109375 to 0.109375
- bias: float32 [128], P('chan'), may hold values from -3 to 3
- cotangent: bfloat16 [16, 256, 128, 128], P(None, 'space', 'chan'), may hold values from -6 to 6
Outputs:
- output: bfloat16 [16, 256, 128, 128], P(None, 'space', 'chan')
- volume_grad: bfloat16 [16, 256, 128, 128], P(None, 'space', 'chan')
The draws below stay inside these ranges and needn't reach their ends.
All inputs are finite; a program needn't handle non-finite values.
Results may differ from the reference program's by a relative error of at most 0.001.
Values may be sent and summed in bfloat16 or wider, within the bound.
No kernel may reach another device: no remote copies, remote signals or barrier semaphores. Data moves between devices by JAX's collectives and lax.ppermute only.
A program may use at most 128 MiB of HBM per device.

```python
import jax
import jax.numpy as jnp

C = 128
X = 16
Z = 128
ROWS = 256


def levels(rng, dims, pieces, low, top_value):
    def one(axis_at, shards_of):
        heights = jax.random.uniform(jax.random.fold_in(jax.random.fold_in(rng, 6), axis_at), (shards_of,), jnp.float32, low / len(pieces), top_value / len(pieces))
        return jnp.repeat(jnp.exp(heights), dims[axis_at] // shards_of).reshape((-1,) + (1,) * (len(dims) - axis_at - 1))

    factor_of = one(*pieces[0])
    for cut in pieces[1:]:
        factor_of = factor_of * one(*cut)
    return factor_of


def noise(own_key, dims, spread, bound, shards=(), kind=jnp.bfloat16):
    drawn = spread * jax.random.normal(own_key, dims, jnp.float32)
    if shards:
        drawn = drawn * levels(own_key, dims, shards, -0.22, 0.18)
    return jnp.clip(drawn, -bound, bound).astype(kind)


def setup_inputs(seed: int = 0) -> dict:
    key_of = jax.random.split(jax.random.key(seed), 5)
    return {
        "volume": noise(key_of[0], (X, ROWS, C, Z), 1.0, 6.0, ((1, 64), (2, 4))),
        "kernel": noise(key_of[1], (27, C, C), (27 * C) ** -0.5, 0.109375, ((2, 4),)),
        "bias": noise(key_of[2], (C,), 0.5, 3.0, ((0, 4),), jnp.float32),
        "cotangent": noise(key_of[3], (X, ROWS, C, Z), 1.0, 6.0, ((1, 64), (2, 4))),
    }


def shifted_terms(padded, weights, forward, total):
    planes = padded.shape[0] - 2
    rows = padded.shape[1] - 2
    columns = padded.shape[3] - 2
    for offset in range(27):
        steps_at = (offset // 9, (offset // 3) % 3, offset % 3)
        if not forward:
            steps_at = (2 - steps_at[0], 2 - steps_at[1], 2 - steps_at[2])
        window = padded[steps_at[0]:steps_at[0] + planes, steps_at[1]:steps_at[1] + rows, :, steps_at[2]:steps_at[2] + columns]
        window = window.astype(jnp.float32)
        weight_now = weights[offset].astype(jnp.float32)
        if forward:
            total = total + jnp.einsum("xyiz,io->xyoz", window, weight_now)
        else:
            total = total + jnp.einsum("xyoz,io->xyiz", window, weight_now)
    return total


def reference(volume, kernel, bias, cotangent):
    padded = jnp.pad(volume, ((1, 1), (1, 1), (0, 0), (1, 1)))
    start = jnp.zeros(volume.shape, jnp.float32) + bias[None, None, :, None]
    output = shifted_terms(padded, kernel, True, start).astype(jnp.bfloat16)
    padded_grad = jnp.pad(cotangent, ((1, 1), (1, 1), (0, 0), (1, 1)))
    volume_grad = shifted_terms(padded_grad, kernel, False, jnp.zeros(volume.shape, jnp.float32))
    return output, volume_grad.astype(jnp.bfloat16)
```

```python
import jax
import jax.numpy as jnp
from jax import lax
from jax.experimental import pallas as pl
from jax.experimental.pallas import tpu as pltpu
from jax.sharding import PartitionSpec as P


MIB = 1024 * 1024
BF16 = jnp.bfloat16
ANY = pl.BlockSpec(memory_space=pl.ANY)
HBM = pl.BlockSpec(memory_space=pltpu.HBM)
VMEM = pl.BlockSpec(memory_space=pltpu.VMEM)
SMEM = pl.BlockSpec(memory_space=pltpu.SMEM)


def shifted(x, steps):
    count = lax.axis_size("chan")
    return lax.ppermute(x, "chan", [(i, (i + steps) % count) for i in range(count)])


def swapped_rows(on_chip, off_chip):
    count = lax.axis_size("space")
    near = [(i, i ^ 1) for i in range(count)]
    far = [(i, i - 1 if i % 2 == 0 else i + 1) for i in range(1, count - 1)]
    return lax.ppermute(on_chip, "space", near), lax.ppermute(off_chip, "space", far)


def copies(plan, sems):
    started = []
    for n, (source, target) in enumerate(plan):
        copy = pltpu.make_async_copy(source, target, sems.at[n])
        copy.start()
        started.append(copy)
    return started


def pack_own(volume, cotangent):
    planes, rows, part, cells = volume.shape

    def body(v, c, ev, ec, sems):
        plan = []
        for x, edge in ((v, ev), (c, ec)):
            plan.append((x.at[:, 0], edge.at[0]))
            plan.append((x.at[:, rows - 1], edge.at[1]))
        for copy in copies(plan, sems):
            copy.wait()

    out = jax.ShapeDtypeStruct((2, planes, part, cells), BF16)
    return pl.pallas_call(
        body,
        out_shape=(out, out),
        in_specs=[HBM, HBM],
        out_specs=[VMEM] * 2,
        scratch_shapes=[pltpu.SemaphoreType.DMA((4,))],
        compiler_params=pltpu.CompilerParams(vmem_limit_bytes=2 * MIB),
        name="pack_own",
    )(volume, cotangent)


def pack_near(core, volume, cotangent, vol_near, cot_near):
    planes, rows, part, cells = volume.shape
    inside = rows - 2

    def body(core_ref, v, c, vn, cn, ev, ec, m_up, m_down, on_chip, off_chip, sems):
        inner = jnp.where(core_ref[0] == 0, rows - 1, 0)
        outer = rows - 1 - inner
        plan = []
        for x, edge in ((vn, ev), (cn, ec)):
            plan.append((x.at[:, 0], edge.at[0]))
            plan.append((x.at[:, rows - 1], edge.at[1]))
        for r in range(inside):
            for n, x in enumerate((c, vn)):
                plan.append((x.at[:, 1 + r], m_up.at[n * inside + r]))
            for n, x in enumerate((v, cn)):
                plan.append((x.at[:, 1 + r], m_down.at[n * inside + r]))
        for n, x in enumerate((v, c, vn, cn)):
            plan.append((x.at[:, inner], on_chip.at[n]))
            plan.append((x.at[:, outer], off_chip.at[n]))
        for copy in copies(plan, sems):
            copy.wait()

    def out(n):
        return jax.ShapeDtypeStruct((n, planes, part, cells), BF16)

    return pl.pallas_call(
        body,
        out_shape=(out(2), out(2), out(2 * inside), out(2 * inside), out(4), out(4)),
        in_specs=[SMEM, HBM, HBM, ANY, ANY],
        out_specs=[VMEM] * 6,
        scratch_shapes=[pltpu.SemaphoreType.DMA((12 + 4 * inside,))],
        compiler_params=pltpu.CompilerParams(vmem_limit_bytes=6 * MIB),
        name="pack_near",
    )(core, volume, cotangent, vol_near, cot_near)


def pack_far(core, blocks):
    _, planes, part, cells = blocks[0].shape
    count = len(blocks)

    def body(core_ref, *refs):
        *held, on_chip, off_chip, sems = refs
        side = jnp.where(core_ref[0] == 0, 1, 0)
        plan = []
        for n, x in enumerate(held):
            plan.append((x.at[side], on_chip.at[n]))
            plan.append((x.at[1 - side], off_chip.at[n]))
        for copy in copies(plan, sems):
            copy.wait()

    out = jax.ShapeDtypeStruct((count, planes, part, cells), BF16)
    return pl.pallas_call(
        body,
        out_shape=(out, out),
        in_specs=[SMEM, *[ANY] * count],
        out_specs=[VMEM] * 2,
        scratch_shapes=[pltpu.SemaphoreType.DMA((2 * count,))],
        compiler_params=pltpu.CompilerParams(vmem_limit_bytes=4 * MIB),
        name="pack_far",
    )(core, *blocks)


def pack_taps(own, size):
    taps, outs, chans = own.shape
    part = chans // size
    groups = -(-taps // size)

    def body(own_ref, send_ref):
        empty = jnp.zeros((outs, part), jnp.float32)
        for g in range(groups):
            quad = [
                own_ref[taps - 1 - t].astype(jnp.float32) if t < taps else None
                for t in range(g * size, (g + 1) * size)
            ]
            for j in range(size):
                pieces = [empty if q is None else q[:, j * part : (j + 1) * part] for q in quad]
                send_ref[j, g] = jnp.concatenate(pieces, axis=1).astype(BF16)

    return pl.pallas_call(
        body,
        out_shape=jax.ShapeDtypeStruct((size, groups, outs, chans), BF16),
        in_specs=[VMEM],
        out_specs=VMEM,
        compiler_params=pltpu.CompilerParams(vmem_limit_bytes=4 * MIB),
        name="pack_taps",
    )(own)


def weights(own, received, turns):
    taps, outs, chans = own.shape
    size, groups = received.shape[:2]
    part = chans // size
    half = chans // 2

    def body(turn_ref, own_ref, got_ref, ahead_a, ahead_b, back_a, back_b):
        low = lax.broadcasted_iota(jnp.int32, (outs, chans), 1) < half

        def put(refs, tiles):
            for at in range(0, 9, 2):
                for c in range(3):
                    here = slice(c * outs, (c + 1) * outs)
                    even = tiles[3 * at + c]
                    if at == 8:
                        refs[0][here, at * half :] = even[:, :half].astype(BF16)
                        refs[1][here, at * half :] = even[:, half:].astype(BF16)
                        continue
                    odd = tiles[3 * at + 3 + c]
                    both = slice(at * half, (at + 2) * half)
                    first = jnp.where(low, even, pltpu.roll(odd, half, 1))
                    second = jnp.where(low, pltpu.roll(even, half, 1), odd)
                    refs[0][here, both] = first.astype(BF16)
                    refs[1][here, both] = second.astype(BF16)

        tiles = [pltpu.roll(own_ref[t].astype(jnp.float32), turn_ref[0], 1) for t in range(taps)]
        put((ahead_a, ahead_b), tiles)
        tiles = []
        for g in range(groups):
            tile = jnp.concatenate([got_ref[s, g] for s in range(size)], axis=0)
            tile = pltpu.roll(tile.astype(jnp.float32).T, turn_ref[1], 1)
            tiles += [tile[t * part : (t + 1) * part] for t in range(size)]
        put((back_a, back_b), tiles)

    out = jax.ShapeDtypeStruct((3 * outs, 9 * half), BF16)
    return pl.pallas_call(
        body,
        out_shape=(out,) * 4,
        in_specs=[SMEM, VMEM, VMEM],
        out_specs=[VMEM] * 4,
        compiler_params=pltpu.CompilerParams(vmem_limit_bytes=6 * MIB),
        name="weights",
    )(turns, own, received)


def convolve(x_ref, w_ref, start, o_ref):
    planes, rows, outs, cells = o_ref.shape
    chans = x_ref.shape[1] // (rows + 2)
    wide = 2 * cells
    lane = lax.broadcasted_iota(jnp.int32, (outs, wide), 1) % cells
    first = lane == 0
    last = lane == cells - 1

    def plane(p, carry):
        for r in range(0, rows, 2):
            halves = []
            for rr in (r, r + 1):
                stack = [x_ref[p + a, rr * chans : (rr + 3) * chans] for a in range(3)]
                halves.append(jnp.concatenate(stack, axis=0))
            data = jnp.concatenate(halves, axis=1)
            sums = jnp.dot(w_ref[...], data, preferred_element_type=jnp.float32)
            total = sums[outs : 2 * outs]
            total = total + jnp.where(first, 0.0, pltpu.roll(sums[:outs], 1, 1))
            total = total + jnp.where(last, 0.0, pltpu.roll(sums[2 * outs :], wide - 1, 1))
            for n in range(2):
                part = total[:, n * cells : (n + 1) * cells]
                if start is not None:
                    part = part + start(p, r + n)
                o_ref[p, r + n] = part.astype(o_ref.dtype)
        return carry

    lax.fori_loop(0, planes, plane, 0, unroll=8)


def stage(core, parts, tables, starts, dtype, shape, fixed=()):
    planes, rows, part, cells = shape
    operands = []
    for plan in parts:
        for block in plan:
            for x, _ in block:
                if not any(x is y for y in operands):
                    operands.append(x)
    count = len(parts[0])
    chans = count * part

    def place(x):
        return [i for i, y in enumerate(operands) if y is x][0]

    def body(core_ref, *refs):
        held = refs[: len(operands)]
        w_refs = refs[len(operands) : len(operands) + 2]
        s_refs = refs[len(operands) + 2 : len(operands) + 2 + len(starts)]
        o_refs = refs[len(operands) + 2 + len(starts) :][:2]
        *x_refs, sems = refs[len(operands) + 4 + len(starts) :]
        upper = core_ref[0] == 0
        inner = jnp.where(upper, rows + 1, 0)
        outer = rows + 1 - inner
        pending = []
        for n, (x_ref, plan) in enumerate(zip(x_refs, parts)):
            work = []
            for s in range(count):
                for r, (x, index) in enumerate(plan[s]):
                    at = [inner, outer, *range(1, rows + 1)][r]
                    base = at * chans + s * part
                    if r < 2:
                        base = pl.multiple_of(base, part)
                    target = x_ref.at[pl.ds(1, planes), pl.ds(base, part)]
                    work.append((held[place(x)].at[index], target))
            pending.append(copies(work, sems.at[n]))
        zero = jnp.zeros((x_refs[0].shape[1], cells), BF16)
        for x_ref in x_refs:
            x_ref[0] = zero
            x_ref[planes + 1] = zero
        for n in range(2):
            for copy in pending[n]:
                copy.wait()
            begin = None
            if n < len(starts):
                if len(starts) == 1:
                    begin = lambda p, r: s_refs[0][...]
                else:
                    begin = lambda p, r, n=n: s_refs[n][p, r]
            convolve(x_refs[n], w_refs[n], begin, o_refs[n])

    out = jax.ShapeDtypeStruct(shape, dtype)
    padded = pltpu.VMEM((planes + 2, (rows + 2) * chans, cells), BF16)
    places = [HBM if any(x is y for y in fixed) else ANY for x in operands]
    return pl.pallas_call(
        body,
        out_shape=(out, out),
        in_specs=[SMEM, *places, *[VMEM] * (2 + len(starts))],
        out_specs=[VMEM, VMEM],
        scratch_shapes=[padded, padded, pltpu.SemaphoreType.DMA((2, count * (rows + 2)))],
        compiler_params=pltpu.CompilerParams(vmem_limit_bytes=12 * MIB),
        cost_estimate=pl.CostEstimate(
            flops=4 * 27 * chans * part * planes * rows * cells,
            bytes_accessed=6 * MIB,
            transcendentals=0,
        ),
    )(core, *operands, *tables, *starts)


def per_device(volume, kernel, bias, cotangent):
    size = lax.axis_size("chan")
    me = lax.axis_index("chan")
    core = (lax.axis_index("space") % 2).astype(jnp.int32).reshape(1)
    _, rows, part, cells = volume.shape
    every = slice(None)

    vol_left = shifted(volume, 1)
    cot_right = shifted(cotangent, -1)
    vol_edge, cot_edge = pack_own(volume, cotangent)
    cot_left_edge = shifted(cot_edge, 1)
    vol_right_edge = shifted(vol_edge, -1)
    own = jnp.swapaxes(kernel, 1, 2)
    received = lax.all_to_all(pack_taps(own, size), "chan", 0, 0, tiled=True)

    vol_edge, cot_edge, mid_up, mid_down, on_chip, off_chip = pack_near(
        core, volume, cotangent, vol_left, cot_right
    )
    vol_edge, cot_edge = shifted(vol_edge, 1), shifted(cot_edge, -1)
    mid_up, mid_down = shifted(mid_up, 1), shifted(mid_down, -1)
    near = swapped_rows(on_chip, off_chip)

    turn = (size - me) % size
    turns = jnp.stack([(turn + 1) % size, turn]).astype(jnp.int32) * part
    ahead_a, ahead_b, back_a, back_b = weights(own, received, turns)

    on_chip, off_chip = pack_far(core, (vol_right_edge, cot_left_edge, vol_edge, cot_edge))
    far = swapped_rows(on_chip, off_chip)

    def whole(x, pair, n):
        return [(pair[0], n), (pair[1], n), *[(x, (every, r)) for r in range(rows)]]

    def split(edge, middle, half, pair, n):
        inner = [(middle, half * (rows - 2) + r) for r in range(rows - 2)]
        return [(pair[0], n), (pair[1], n), (edge, 0), *inner, (edge, 1)]

    wide = jnp.broadcast_to(bias[:, None], (bias.shape[0], cells))
    sums = stage(
        core,
        [
            [whole(vol_left, near, 2), whole(volume, near, 0)],
            [whole(cotangent, near, 1), whole(cot_right, near, 3)],
        ],
        (ahead_a, back_a),
        (wide,),
        jnp.float32,
        volume.shape,
        (volume, cotangent),
    )
    return stage(
        core,
        [
            [split(vol_right_edge, mid_down, 0, far, 0), split(vol_edge, mid_up, 1, far, 2)],
            [split(cot_edge, mid_down, 1, far, 3), split(cot_left_edge, mid_up, 0, far, 1)],
        ],
        (ahead_b, back_b),
        sums,
        BF16,
        volume.shape,
    )


def solution(mesh):
    spec = P(None, "space", "chan", None)

    return jax.shard_map(
        per_device,
        mesh=mesh,
        in_specs=(spec, P(None, None, "chan"), P("chan"), spec),
        out_specs=(spec, spec),
        check_vma=False,
    )
```

```python
import jax
import jax.numpy as jnp
from jax import lax
from jax.experimental import pallas as pl
from jax.experimental.pallas import tpu as pltpu
from jax.sharding import PartitionSpec as P


MIB = 1024 * 1024
BF16 = jnp.bfloat16
VMEM = pl.BlockSpec(memory_space=pltpu.VMEM)
SMEM = pl.BlockSpec(memory_space=pltpu.SMEM)


def shifted(x, steps):
    count = lax.axis_size("chan")
    return lax.ppermute(x, "chan", [(i, (i + steps) % count) for i in range(count)])


def swapped_rows(on_chip, off_chip):
    count = lax.axis_size("space")
    near = [(i, i ^ 1) for i in range(count)]
    far = [(i, i - 1 if i % 2 == 0 else i + 1) for i in range(1, count - 1)]
    return lax.ppermute(on_chip, "space", near), lax.ppermute(off_chip, "space", far)


def pack_own(core, me, volume, cotangent):
    planes, rows, part, cells = volume.shape

    def body(core_ref, me_ref, v, c, ev, ec):
        for x, edge in ((v, ev), (c, ec)):
            edge[0] = x[:, 0]
            edge[1] = x[:, rows - 1]

    out = jax.ShapeDtypeStruct((2, planes, part, cells), BF16)
    return pl.pallas_call(
        body,
        out_shape=(out, out),
        in_specs=[SMEM, SMEM, VMEM, VMEM],
        out_specs=[VMEM] * 2,
        compiler_params=pltpu.CompilerParams(vmem_limit_bytes=4 * MIB),
        name="pack_own",
    )(core, me, volume, cotangent)


def pack_near(core, volume, cotangent, vol_near, cot_near):
    planes, rows, part, cells = volume.shape
    inside = rows - 2

    def body(core_ref, v, c, vn, cn, ev, ec, m_up, m_down, on_chip, off_chip):
        inner = jnp.where(core_ref[0] == 0, rows - 1, 0)
        outer = rows - 1 - inner
        for x, edge in ((vn, ev), (cn, ec)):
            edge[0] = x[:, 0]
            edge[1] = x[:, rows - 1]
        for r in range(inside):
            for n, x in enumerate((c, vn)):
                m_up[n * inside + r] = x[:, 1 + r]
            for n, x in enumerate((v, cn)):
                m_down[n * inside + r] = x[:, 1 + r]
        for n, x in enumerate((v, c, vn, cn)):
            on_chip[n] = x[:, inner]
            off_chip[n] = x[:, outer]

    def out(n):
        return jax.ShapeDtypeStruct((n, planes, part, cells), BF16)

    return pl.pallas_call(
        body,
        out_shape=(out(2), out(2), out(2 * inside), out(2 * inside), out(4), out(4)),
        in_specs=[SMEM, *[VMEM] * 4],
        out_specs=[VMEM] * 6,
        compiler_params=pltpu.CompilerParams(vmem_limit_bytes=8 * MIB),
        name="pack_near",
    )(core, volume, cotangent, vol_near, cot_near)


def pack_far(core, blocks):
    _, planes, part, cells = blocks[0].shape
    count = len(blocks)

    def body(core_ref, *refs):
        *held, on_chip, off_chip = refs
        side = jnp.where(core_ref[0] == 0, 1, 0)
        for n, x in enumerate(held):
            on_chip[n] = x[side]
            off_chip[n] = x[1 - side]

    out = jax.ShapeDtypeStruct((count, planes, part, cells), BF16)
    return pl.pallas_call(
        body,
        out_shape=(out, out),
        in_specs=[SMEM, *[VMEM] * count],
        out_specs=[VMEM] * 2,
        compiler_params=pltpu.CompilerParams(vmem_limit_bytes=6 * MIB),
        name="pack_far",
    )(core, *blocks)


def pack_taps(place, own, size):
    taps, outs, chans = own.shape
    part = chans // size
    groups = -(-taps // size)

    def body(place_ref, own_ref, *send_refs):
        turn = lax.rem(size - place_ref[0], size) * part
        empty = jnp.zeros((outs, chans), jnp.float32)
        for g in range(groups):
            quad = [
                pltpu.roll(own_ref[taps - 1 - t].astype(jnp.float32), turn, 1) if t < taps else empty
                for t in range(g * size, (g + 1) * size)
            ]
            for j in range(size):
                pieces = [q[:, j * part : (j + 1) * part] for q in quad]
                send_refs[j][g] = jnp.concatenate(pieces, axis=1).astype(BF16)

    return pl.pallas_call(
        body,
        out_shape=(jax.ShapeDtypeStruct((groups, outs, chans), BF16),) * size,
        in_specs=[SMEM, VMEM],
        out_specs=[VMEM] * size,
        compiler_params=pltpu.CompilerParams(vmem_limit_bytes=4 * MIB),
        name="pack_taps",
    )(place, own)


def weights(place, own, received, bias, cells):
    taps, outs, chans = own.shape
    size, groups = len(received), received[0].shape[0]
    part = chans // size
    half = chans // 2

    def body(place_ref, own_ref, *refs):
        got_refs = refs[:size]
        bias_ref, ahead_a, ahead_b, back_a, back_b, wide_ref = refs[size:]
        turn = lax.rem(size - place_ref[0] + 1, size) * part
        shape = (outs, outs)
        same = lax.broadcasted_iota(jnp.int32, shape, 0) == lax.broadcasted_iota(jnp.int32, shape, 1)
        column = jnp.sum(jnp.where(same, bias_ref[...], 0.0), axis=1, keepdims=True)
        wide_ref[...] = jnp.broadcast_to(column, wide_ref.shape)
        low = lax.broadcasted_iota(jnp.int32, (outs, chans), 1) < half

        def put(refs, tiles):
            for at in range(0, 9, 2):
                for c in range(3):
                    here = slice(c * outs, (c + 1) * outs)
                    even = tiles[3 * at + c]
                    if at == 8:
                        refs[0][here, at * half :] = even[:, :half].astype(BF16)
                        refs[1][here, at * half :] = even[:, half:].astype(BF16)
                        continue
                    odd = tiles[3 * at + 3 + c]
                    both = slice(at * half, (at + 2) * half)
                    first = jnp.where(low, even, pltpu.roll(odd, half, 1))
                    second = jnp.where(low, pltpu.roll(even, half, 1), odd)
                    refs[0][here, both] = first.astype(BF16)
                    refs[1][here, both] = second.astype(BF16)

        tiles = [pltpu.roll(own_ref[t].astype(jnp.float32), turn, 1) for t in range(taps)]
        put((ahead_a, ahead_b), tiles)
        tiles = []
        for g in range(groups):
            tile = jnp.concatenate([got[g] for got in got_refs], axis=0)
            tile = tile.astype(jnp.float32).T
            tiles += [tile[t * part : (t + 1) * part] for t in range(size)]
        put((back_a, back_b), tiles)

    out = jax.ShapeDtypeStruct((3 * outs, 9 * half), BF16)
    return pl.pallas_call(
        body,
        out_shape=(*[out] * 4, jax.ShapeDtypeStruct((outs, cells), jnp.float32)),
        in_specs=[SMEM, *[VMEM] * (size + 2)],
        out_specs=[VMEM] * 5,
        compiler_params=pltpu.CompilerParams(vmem_limit_bytes=6 * MIB),
        name="weights",
    )(place, own, *received, bias.reshape(1, outs))


def convolve(source, w_ref, start, o_ref):
    planes, rows, outs, cells = o_ref.shape
    wide = 2 * cells
    lane = lax.broadcasted_iota(jnp.int32, (outs, wide), 1) % cells
    first = lane == 0
    last = lane == cells - 1
    step = w_ref.shape[1] // 3
    for p in range(planes):
        low, high = max(p - 1, 0), min(p + 1, planes - 1)
        table = w_ref[:, (low - p + 1) * step : (high - p + 2) * step]
        for r in range(0, rows, 2):
            halves = []
            for rr in (r, r + 1):
                stack = []
                for at in range(low, high + 1):
                    for b in range(3):
                        stack += source(at, rr + b)
                halves.append(jnp.concatenate(stack, axis=0))
            data = jnp.concatenate(halves, axis=1)
            sums = jnp.dot(table, data, preferred_element_type=jnp.float32)
            total = sums[outs : 2 * outs]
            total = total + jnp.where(first, 0.0, pltpu.roll(sums[:outs], 1, 1))
            total = total + jnp.where(last, 0.0, pltpu.roll(sums[2 * outs :], wide - 1, 1))
            for n in range(2):
                piece = total[:, n * cells : (n + 1) * cells]
                if start is not None:
                    piece = piece + start(p, r + n)
                o_ref[p, r + n] = piece.astype(o_ref.dtype)


def stage(core, parts, tables, starts, dtype, shape):
    planes, rows, part, cells = shape
    operands = []
    for plan in parts:
        for on_chip, off_chip, _, inner in plan:
            for x in (on_chip, off_chip, *[x for x, _, _ in inner]):
                if not any(x is y for y in operands):
                    operands.append(x)
    count = len(parts[0])

    def place(x):
        return [i for i, y in enumerate(operands) if y is x][0]

    def body(core_ref, *refs):
        held = refs[: len(operands)]
        w_refs = refs[len(operands) : len(operands) + 2]
        s_refs = refs[len(operands) + 2 : len(operands) + 2 + len(starts)]
        o_refs = refs[len(operands) + 2 + len(starts) :][:2]
        low_ref, high_ref = refs[len(operands) + 4 + len(starts) :]
        places = [(block[0], block[1], block[2]) for plan in parts for block in plan]

        @pl.when(core_ref[0] == 0)
        def _():
            for i, (on_chip, off_chip, n) in enumerate(places):
                high_ref[i] = held[place(on_chip)][n]
                low_ref[i] = held[place(off_chip)][n]

        @pl.when(core_ref[0] != 0)
        def _():
            for i, (on_chip, off_chip, n) in enumerate(places):
                low_ref[i] = held[place(on_chip)][n]
                high_ref[i] = held[place(off_chip)][n]

        for n in range(2):

            def source(p, r, n=n):
                if r == 0:
                    return [low_ref[n * count + s, p] for s in range(count)]
                if r == rows + 1:
                    return [high_ref[n * count + s, p] for s in range(count)]
                found = []
                for s in range(count):
                    x, before, at = parts[n][s][3][r - 1]
                    ref = held[place(x)]
                    found.append(ref[at, p] if before else ref[p, at])
                return found

            begin = None
            if n < len(starts):
                if len(starts) == 1:
                    begin = lambda p, r: s_refs[0][...]
                else:
                    begin = lambda p, r, n=n: s_refs[n][p, r]
            convolve(source, w_refs[n], begin, o_refs[n])

    out = jax.ShapeDtypeStruct(shape, dtype)
    edge = pltpu.VMEM((2 * count, planes, part, cells), BF16)
    return pl.pallas_call(
        body,
        out_shape=(out, out),
        in_specs=[SMEM, *[VMEM] * (len(operands) + 2 + len(starts))],
        out_specs=[VMEM, VMEM],
        scratch_shapes=[edge, edge],
        compiler_params=pltpu.CompilerParams(vmem_limit_bytes=14 * MIB),
        cost_estimate=pl.CostEstimate(
            flops=4 * 27 * count * part * part * planes * rows * cells,
            bytes_accessed=6 * MIB,
            transcendentals=0,
        ),
    )(core, *operands, *tables, *starts)


def per_device(volume, kernel, bias, cotangent):
    size = lax.axis_size("chan")
    me = lax.axis_index("chan").astype(jnp.int32).reshape(1)
    core = (lax.axis_index("space") % 2).astype(jnp.int32).reshape(1)
    _, rows, _, cells = volume.shape

    vol_left = shifted(volume, 1)
    cot_right = shifted(cotangent, -1)
    vol_edge, cot_edge = pack_own(core, me, volume, cotangent)
    cot_left_edge = shifted(cot_edge, 1)
    vol_right_edge = shifted(vol_edge, -1)
    own = jnp.swapaxes(kernel, 1, 2)
    sent = pack_taps(me, own, size)
    received = [sent[0], *[shifted(sent[size - d], -d) for d in range(1, size)]]

    vol_edge, cot_edge, mid_up, mid_down, on_chip, off_chip = pack_near(core, volume, cotangent, vol_left, cot_right)
    vol_edge, cot_edge = shifted(vol_edge, 1), shifted(cot_edge, -1)
    mid_up, mid_down = shifted(mid_up, 1), shifted(mid_down, -1)
    near = swapped_rows(on_chip, off_chip)

    ahead_a, ahead_b, back_a, back_b, wide = weights(me, own, received, bias, cells)

    on_chip, off_chip = pack_far(core, (vol_right_edge, cot_left_edge, vol_edge, cot_edge))
    far = swapped_rows(on_chip, off_chip)

    def whole(x, pair, n):
        return (*pair, n, [(x, False, r) for r in range(rows)])

    def split(edge, middle, half, pair, n):
        inner = [(middle, True, half * (rows - 2) + r) for r in range(rows - 2)]
        return (*pair, n, [(edge, True, 0), *inner, (edge, True, 1)])

    sums = stage(
        core,
        [[whole(vol_left, near, 2), whole(volume, near, 0)], [whole(cotangent, near, 1), whole(cot_right, near, 3)]],
        (ahead_a, back_a),
        (wide,),
        jnp.float32,
        volume.shape,
    )
    return stage(
        core,
        [
            [split(vol_right_edge, mid_down, 0, far, 0), split(vol_edge, mid_up, 1, far, 2)],
            [split(cot_edge, mid_down, 1, far, 3), split(cot_left_edge, mid_up, 0, far, 1)],
        ],
        (ahead_b, back_b),
        sums,
        BF16,
        volume.shape,
    )


def solution(mesh):
    spec = P(None, "space", "chan", None)

    return jax.shard_map(
        per_device,
        mesh=mesh,
        in_specs=(spec, P(None, None, "chan"), P("chan"), spec),
        out_specs=(spec, spec),
        check_vma=False,
    )
```

```python
import jax
import jax.numpy as jnp
from jax import lax
from jax.experimental import pallas as pl
from jax.experimental.pallas import tpu as pltpu
from jax.sharding import PartitionSpec as P


MIB = 1024 * 1024
BF16 = jnp.bfloat16
VMEM = pl.BlockSpec(memory_space=pltpu.VMEM)
SMEM = pl.BlockSpec(memory_space=pltpu.SMEM)


def shifted(x, steps):
    count = lax.axis_size("chan")
    return lax.ppermute(x, "chan", [(i, (i + steps) % count) for i in range(count)])


def swapped_rows(on_chip, off_chip):
    count = lax.axis_size("space")
    near = [(i, i ^ 1) for i in range(count)]
    far = [(i, i - 1 if i % 2 == 0 else i + 1) for i in range(1, count - 1)]
    off_chip = lax.ppermute(off_chip, "space", far)
    on_chip = lax.ppermute(on_chip, "space", near)
    return on_chip, off_chip


def pack_own(core, me, volume, cotangent):
    planes, rows, part, cells = volume.shape

    def body(core_ref, me_ref, v, c, ev, ec, on_chip, off_chip):
        side = jnp.where(core_ref[0] == 0, 1, 0)
        for n, (x, edge) in enumerate(((v, ev), (c, ec))):
            edge[0] = x[:, 0]
            edge[1] = x[:, rows - 1]
            on_chip[n] = x[:, side * (rows - 1)]
            off_chip[n] = x[:, (1 - side) * (rows - 1)]

    out = jax.ShapeDtypeStruct((2, planes, part, cells), BF16)
    return pl.pallas_call(
        body,
        out_shape=(out,) * 4,
        in_specs=[SMEM, SMEM, VMEM, VMEM],
        out_specs=[VMEM] * 4,
        compiler_params=pltpu.CompilerParams(vmem_limit_bytes=4 * MIB),
        name="pack_own",
    )(core, me, volume, cotangent)


def pack_forward(volume, cotangent, vol_near, cot_near):
    planes, rows, part, cells = volume.shape
    inside = rows - 2

    def body(v, c, vn, cn, ev, ec, m_up, m_down):
        for x, edge in ((vn, ev), (cn, ec)):
            edge[0] = x[:, 0]
            edge[1] = x[:, rows - 1]
        for r in range(inside):
            for n, x in enumerate((c, vn)):
                m_up[n * inside + r] = x[:, 1 + r]
            for n, x in enumerate((v, cn)):
                m_down[n * inside + r] = x[:, 1 + r]

    def out(n):
        return jax.ShapeDtypeStruct((n, planes, part, cells), BF16)

    return pl.pallas_call(
        body,
        out_shape=(out(2), out(2), out(2 * inside), out(2 * inside)),
        in_specs=[VMEM] * 4,
        out_specs=[VMEM] * 4,
        compiler_params=pltpu.CompilerParams(vmem_limit_bytes=8 * MIB),
        name="pack_forward",
    )(volume, cotangent, vol_near, cot_near)


def pack_rows(core, wholes, edges):
    planes, part, cells = edges[0].shape[1:]
    count = len(wholes) + len(edges)

    def body(core_ref, *refs):
        *held, on_chip, off_chip = refs
        side = jnp.where(core_ref[0] == 0, 1, 0)
        for n, x in enumerate(held):
            if n < len(wholes):
                rows = x.shape[1]
                on_chip[n] = x[:, side * (rows - 1)]
                off_chip[n] = x[:, (1 - side) * (rows - 1)]
            else:
                on_chip[n] = x[side]
                off_chip[n] = x[1 - side]

    out = jax.ShapeDtypeStruct((count, planes, part, cells), BF16)
    return pl.pallas_call(
        body,
        out_shape=(out, out),
        in_specs=[SMEM, *[VMEM] * count],
        out_specs=[VMEM] * 2,
        compiler_params=pltpu.CompilerParams(vmem_limit_bytes=8 * MIB),
    )(core, *wholes, *edges)


def pack_taps(place, own, bias, size, cells):
    taps, outs, chans = own.shape
    part = chans // size
    groups = -(-taps // size)

    def body(place_ref, own_ref, bias_ref, wide_ref, *send_refs):
        shape = (outs, outs)
        same = lax.broadcasted_iota(jnp.int32, shape, 0) == lax.broadcasted_iota(jnp.int32, shape, 1)
        column = jnp.sum(jnp.where(same, bias_ref[...], 0.0), axis=1, keepdims=True)
        wide_ref[...] = jnp.broadcast_to(column, wide_ref.shape)
        turn = lax.rem(size - place_ref[0], size) * part
        empty = jnp.zeros((outs, chans), jnp.float32)
        for g in range(groups):
            quad = [
                pltpu.roll(own_ref[taps - 1 - t].astype(jnp.float32), turn, 1) if t < taps else empty
                for t in range(g * size, (g + 1) * size)
            ]
            for j in range(size):
                pieces = [q[:, j * part : (j + 1) * part] for q in quad]
                send_refs[j][g] = jnp.concatenate(pieces, axis=1).astype(BF16)

    return pl.pallas_call(
        body,
        out_shape=(
            jax.ShapeDtypeStruct((outs, cells), jnp.float32),
            *[jax.ShapeDtypeStruct((groups, outs, chans), BF16)] * size,
        ),
        in_specs=[SMEM, VMEM, VMEM],
        out_specs=[VMEM] * (size + 1),
        compiler_params=pltpu.CompilerParams(vmem_limit_bytes=4 * MIB),
        name="pack_taps",
    )(place, own, bias.reshape(1, outs))


def weights(place, own, received):
    taps, outs, chans = own.shape
    size, groups = len(received), received[0].shape[0]
    part = chans // size
    half = chans // 2

    def body(place_ref, own_ref, *refs):
        got_refs = refs[:size]
        ahead_a, ahead_b, back_a, back_b = refs[size:]
        turn = lax.rem(size - place_ref[0] + 1, size) * part
        low = lax.broadcasted_iota(jnp.int32, (outs, chans), 1) < half

        def put(refs, tiles):
            for at in range(0, 9, 2):
                for c in range(3):
                    here = slice(c * outs, (c + 1) * outs)
                    even = tiles[3 * at + c]
                    if at == 8:
                        refs[0][here, at * half :] = even[:, :half].astype(BF16)
                        refs[1][here, at * half :] = even[:, half:].astype(BF16)
                        continue
                    odd = tiles[3 * at + 3 + c]
                    both = slice(at * half, (at + 2) * half)
                    first = jnp.where(low, even, pltpu.roll(odd, half, 1))
                    second = jnp.where(low, pltpu.roll(even, half, 1), odd)
                    refs[0][here, both] = first.astype(BF16)
                    refs[1][here, both] = second.astype(BF16)

        tiles = [pltpu.roll(own_ref[t].astype(jnp.float32), turn, 1) for t in range(taps)]
        put((ahead_a, ahead_b), tiles)
        tiles = []
        for g in range(groups):
            tile = jnp.concatenate([got[g] for got in got_refs], axis=0)
            tile = tile.astype(jnp.float32).T
            tiles += [tile[t * part : (t + 1) * part] for t in range(size)]
        put((back_a, back_b), tiles)

    out = jax.ShapeDtypeStruct((3 * outs, 9 * half), BF16)
    return pl.pallas_call(
        body,
        out_shape=(out,) * 4,
        in_specs=[SMEM, *[VMEM] * (size + 1)],
        out_specs=[VMEM] * 4,
        compiler_params=pltpu.CompilerParams(vmem_limit_bytes=6 * MIB),
        name="weights",
    )(place, own, *received)


def convolve(source, w_ref, start, o_ref):
    planes, rows, outs, cells = o_ref.shape
    wide = 2 * cells
    lane = lax.broadcasted_iota(jnp.int32, (outs, wide), 1) % cells
    first = lane == 0
    last = lane == cells - 1
    step = w_ref.shape[1] // 3
    for p in range(planes):
        low, high = max(p - 1, 0), min(p + 1, planes - 1)
        table = w_ref[:, (low - p + 1) * step : (high - p + 2) * step]
        for r in range(0, rows, 2):
            halves = []
            for rr in (r, r + 1):
                stack = []
                for at in range(low, high + 1):
                    for b in range(3):
                        stack += source(at, rr + b)
                halves.append(jnp.concatenate(stack, axis=0))
            data = jnp.concatenate(halves, axis=1)
            sums = jnp.dot(table, data, preferred_element_type=jnp.float32)
            total = sums[outs : 2 * outs]
            total = total + jnp.where(first, 0.0, pltpu.roll(sums[:outs], 1, 1))
            total = total + jnp.where(last, 0.0, pltpu.roll(sums[2 * outs :], wide - 1, 1))
            for n in range(2):
                piece = total[:, n * cells : (n + 1) * cells]
                if start is not None:
                    piece = piece + start(p, r + n)
                o_ref[p, r + n] = piece.astype(o_ref.dtype)


def stage(core, parts, tables, starts, dtype, shape):
    planes, rows, part, cells = shape
    operands = []
    for plan in parts:
        for on_chip, off_chip, _, inner in plan:
            for x in (on_chip, off_chip, *[x for x, _, _ in inner]):
                if not any(x is y for y in operands):
                    operands.append(x)
    count = len(parts[0])

    def place(x):
        return [i for i, y in enumerate(operands) if y is x][0]

    def body(core_ref, *refs):
        held = refs[: len(operands)]
        w_refs = refs[len(operands) : len(operands) + 2]
        s_refs = refs[len(operands) + 2 : len(operands) + 2 + len(starts)]
        o_refs = refs[len(operands) + 2 + len(starts) :][:2]
        low_ref, high_ref = refs[len(operands) + 4 + len(starts) :]
        places = [(block[0], block[1], block[2]) for plan in parts for block in plan]

        @pl.when(core_ref[0] == 0)
        def _():
            for i, (on_chip, off_chip, n) in enumerate(places):
                high_ref[i] = held[place(on_chip)][n]
                low_ref[i] = held[place(off_chip)][n]

        @pl.when(core_ref[0] != 0)
        def _():
            for i, (on_chip, off_chip, n) in enumerate(places):
                low_ref[i] = held[place(on_chip)][n]
                high_ref[i] = held[place(off_chip)][n]

        for n in range(2):

            def source(p, r, n=n):
                if r == 0:
                    return [low_ref[n * count + s, p] for s in range(count)]
                if r == rows + 1:
                    return [high_ref[n * count + s, p] for s in range(count)]
                found = []
                for s in range(count):
                    x, before, at = parts[n][s][3][r - 1]
                    ref = held[place(x)]
                    found.append(ref[at, p] if before else ref[p, at])
                return found

            begin = None
            if n < len(starts):
                if len(starts) == 1:
                    begin = lambda p, r: s_refs[0][...]
                else:
                    begin = lambda p, r, n=n: s_refs[n][p, r]
            convolve(source, w_refs[n], begin, o_refs[n])

    out = jax.ShapeDtypeStruct(shape, dtype)
    edge = pltpu.VMEM((2 * count, planes, part, cells), BF16)
    return pl.pallas_call(
        body,
        out_shape=(out, out),
        in_specs=[SMEM, *[VMEM] * (len(operands) + 2 + len(starts))],
        out_specs=[VMEM, VMEM],
        scratch_shapes=[edge, edge],
        compiler_params=pltpu.CompilerParams(vmem_limit_bytes=14 * MIB),
        cost_estimate=pl.CostEstimate(
            flops=4 * 27 * count * part * part * planes * rows * cells,
            bytes_accessed=6 * MIB,
            transcendentals=0,
        ),
    )(core, *operands, *tables, *starts)


def per_device(volume, kernel, bias, cotangent):
    size = lax.axis_size("chan")
    me = lax.axis_index("chan").astype(jnp.int32).reshape(1)
    core = (lax.axis_index("space") % 2).astype(jnp.int32).reshape(1)
    _, rows, _, cells = volume.shape

    vol_left = shifted(volume, 1)
    cot_right = shifted(cotangent, -1)
    vol_edge, cot_edge, on_chip, off_chip = pack_own(core, me, volume, cotangent)
    mine = swapped_rows(on_chip, off_chip)
    cot_left_edge = shifted(cot_edge, 1)
    vol_right_edge = shifted(vol_edge, -1)
    own = jnp.swapaxes(kernel, 1, 2)
    wide, *sent = pack_taps(me, own, bias, size, cells)
    received = [sent[0], *[shifted(sent[size - d], -d) for d in range(1, size)]]

    vol_edge, cot_edge, mid_up, mid_down = pack_forward(volume, cotangent, vol_left, cot_right)
    vol_edge, cot_edge = shifted(vol_edge, 1), shifted(cot_edge, -1)
    mid_up, mid_down = shifted(mid_up, 1), shifted(mid_down, -1)
    near = pack_rows(core, (vol_left, cot_right), (vol_right_edge, cot_left_edge))
    near = swapped_rows(*near)

    ahead_a, ahead_b, back_a, back_b = weights(me, own, received)

    far = pack_rows(core, (), (vol_edge, cot_edge))
    far = swapped_rows(*far)

    def whole(x, pair, n):
        return (*pair, n, [(x, False, r) for r in range(rows)])

    def split(edge, middle, half, pair, n):
        inner = [(middle, True, half * (rows - 2) + r) for r in range(rows - 2)]
        return (*pair, n, [(edge, True, 0), *inner, (edge, True, 1)])

    sums = stage(
        core,
        [[whole(vol_left, near, 0), whole(volume, mine, 0)], [whole(cotangent, mine, 1), whole(cot_right, near, 1)]],
        (ahead_a, back_a),
        (wide,),
        jnp.float32,
        volume.shape,
    )
    return stage(
        core,
        [
            [split(vol_right_edge, mid_down, 0, near, 2), split(vol_edge, mid_up, 1, far, 0)],
            [split(cot_edge, mid_down, 1, far, 1), split(cot_left_edge, mid_up, 0, near, 3)],
        ],
        (ahead_b, back_b),
        sums,
        BF16,
        volume.shape,
    )


def solution(mesh):
    spec = P(None, "space", "chan", None)

    return jax.shard_map(
        per_device,
        mesh=mesh,
        in_specs=(spec, P(None, None, "chan"), P("chan"), spec),
        out_specs=(spec, spec),
        check_vma=False,
    )
```

```python
import jax
import jax.numpy as jnp
from jax import lax
from jax.experimental import pallas as pl
from jax.experimental.pallas import tpu as pltpu
from jax.sharding import PartitionSpec as P


MIB = 1024 * 1024
BF16 = jnp.bfloat16
VMEM = pl.BlockSpec(memory_space=pltpu.VMEM)
SMEM = pl.BlockSpec(memory_space=pltpu.SMEM)


INNER_ONE = tuple((0, at) for at in range(8))
INNER_TWO = (*[(1, at) for at in range(9)], (0, 8))
OUTER_ONE = (*[(0, at) for at in range(9)], (1, 1), (1, 4), (1, 7))
OUTER_TWO = tuple((1, at) for at in (0, 2, 3, 5, 6, 8))


def shifted(x, steps):
    count = lax.axis_size("chan")
    return lax.ppermute(x, "chan", [(i, (i + steps) % count) for i in range(count)])


def swapped_rows(on_chip, off_chip):
    count = lax.axis_size("space")
    near = [(i, i ^ 1) for i in range(count)]
    far = [(i, i - 1 if i % 2 == 0 else i + 1) for i in range(1, count - 1)]
    off_chip = lax.ppermute(off_chip, "space", far)
    on_chip = lax.ppermute(on_chip, "space", near)
    return on_chip, off_chip


def pack_forward(volume, cotangent, vol_near, cot_near):
    planes, rows, part, cells = volume.shape
    inside = rows - 2

    def body(v, c, vn, cn, ev, ec, m_up, m_down):
        for x, edge in ((vn, ev), (cn, ec)):
            edge[0] = x[:, 0]
            edge[1] = x[:, rows - 1]
        for r in range(inside):
            for n, x in enumerate((c, vn)):
                m_up[n * inside + r] = x[:, 1 + r]
            for n, x in enumerate((v, cn)):
                m_down[n * inside + r] = x[:, 1 + r]

    def out(n):
        return jax.ShapeDtypeStruct((n, planes, part, cells), BF16)

    return pl.pallas_call(
        body,
        out_shape=(out(2), out(2), out(2 * inside), out(2 * inside)),
        in_specs=[VMEM] * 4,
        out_specs=[VMEM] * 4,
        compiler_params=pltpu.CompilerParams(vmem_limit_bytes=8 * MIB),
        name="pack_forward",
    )(volume, cotangent, vol_near, cot_near)


def pack_rows(core, wholes, edges):
    planes, part, cells = edges[0].shape[1:]
    count = len(wholes) + len(edges)

    def body(core_ref, *refs):
        *held, on_chip, off_chip = refs
        side = jnp.where(core_ref[0] == 0, 1, 0)
        for n, x in enumerate(held):
            if n < len(wholes):
                rows = x.shape[1]
                on_chip[n] = x[:, side * (rows - 1)]
                off_chip[n] = x[:, (1 - side) * (rows - 1)]
            else:
                on_chip[n] = x[side]
                off_chip[n] = x[1 - side]

    out = jax.ShapeDtypeStruct((count, planes, part, cells), BF16)
    return pl.pallas_call(
        body,
        out_shape=(out, out),
        in_specs=[SMEM, *[VMEM] * count],
        out_specs=[VMEM] * 2,
        compiler_params=pltpu.CompilerParams(vmem_limit_bytes=8 * MIB),
    )(core, *wholes, *edges)


def prologue(core, place, volume, cotangent, own, bias, size):
    planes, rows, part, cells = volume.shape
    taps, outs, chans = own.shape
    groups = -(-taps // size)

    def body(core_ref, place_ref, v, c, own_ref, bias_ref, *out_refs):
        ev, ec, on_chip, off_chip, wide_ref, *send_refs = out_refs
        side = jnp.where(core_ref[0] == 0, 1, 0)
        for n, (x, edge) in enumerate(((v, ev), (c, ec))):
            edge[0] = x[:, 0]
            edge[1] = x[:, rows - 1]
            on_chip[n] = x[:, side * (rows - 1)]
            off_chip[n] = x[:, (1 - side) * (rows - 1)]
        shape = (outs, outs)
        same = lax.broadcasted_iota(jnp.int32, shape, 0) == lax.broadcasted_iota(jnp.int32, shape, 1)
        column = jnp.sum(jnp.where(same, bias_ref[...], 0.0), axis=1, keepdims=True)
        wide_ref[...] = jnp.broadcast_to(column, wide_ref.shape)
        turn = lax.rem(size - place_ref[0], size) * part
        empty = jnp.zeros((outs, chans), jnp.float32)
        for g in range(groups):
            quad = [
                pltpu.roll(own_ref[taps - 1 - t].astype(jnp.float32), turn, 1) if t < taps else empty
                for t in range(g * size, (g + 1) * size)
            ]
            for j in range(size):
                pieces = [q[:, j * part : (j + 1) * part] for q in quad]
                send_refs[j][g] = jnp.concatenate(pieces, axis=1).astype(BF16)

    two = jax.ShapeDtypeStruct((2, planes, part, cells), BF16)
    return pl.pallas_call(
        body,
        out_shape=(
            *[two] * 4,
            jax.ShapeDtypeStruct((outs, cells), jnp.float32),
            *[jax.ShapeDtypeStruct((groups, outs, chans), BF16)] * size,
        ),
        in_specs=[SMEM, SMEM, *[VMEM] * 4],
        out_specs=[VMEM] * (size + 5),
        compiler_params=pltpu.CompilerParams(vmem_limit_bytes=61 * MIB + MIB // 2),
        name="prologue",
    )(core, place, volume, cotangent, own, bias.reshape(1, outs))


def weights(place, own, received, layouts):
    taps, outs, chans = own.shape
    size, groups = len(received), received[0].shape[0]
    part = chans // size
    half = chans // 2

    def body(place_ref, own_ref, *refs):
        got_refs = refs[:size]
        table_refs = refs[size:]
        turn = lax.rem(size - place_ref[0] + 1, size) * part
        low = lax.broadcasted_iota(jnp.int32, (outs, chans), 1) < half

        def put(ref, chunks, tiles):
            for c in range(3):
                here = slice(c * outs, (c + 1) * outs)
                for k in range(0, len(chunks), 2):
                    found = []
                    for side, (n, at) in enumerate(chunks[k : k + 2]):
                        tile = tiles[3 * at + c]
                        found.append(tile if n == side else pltpu.roll(tile, half, 1))
                    if len(found) == 2:
                        both = jnp.where(low, *found)
                        ref[here, k * half : (k + 2) * half] = both.astype(BF16)
                    else:
                        ref[here, k * half :] = found[0][:, :half].astype(BF16)

        tiles = [pltpu.roll(own_ref[t].astype(jnp.float32), turn, 1) for t in range(taps)]
        for n, chunks in enumerate(layouts):
            put(table_refs[2 * n], chunks, tiles)
        tiles = []
        for g in range(groups):
            tile = jnp.concatenate([got[g] for got in got_refs], axis=0)
            tile = tile.astype(jnp.float32).T
            tiles += [tile[t * part : (t + 1) * part] for t in range(size)]
        for n, chunks in enumerate(layouts):
            put(table_refs[2 * n + 1], chunks, tiles)

    shapes = [jax.ShapeDtypeStruct((3 * outs, len(chunks) * half), BF16) for chunks in layouts]
    return pl.pallas_call(
        body,
        out_shape=tuple(shape for shape in shapes for _ in range(2)),
        in_specs=[SMEM, *[VMEM] * (size + 1)],
        out_specs=[VMEM] * (2 * len(layouts)),
        compiler_params=pltpu.CompilerParams(vmem_limit_bytes=8 * MIB),
        name="weights",
    )(place, own, *received)


def stage(core, halves, jobs, starts, shape, final):
    planes, rows, part, cells = shape
    outs = part
    wide = 2 * cells
    needed = set()
    for pair, chunks, _ in jobs:
        needed |= {(n, r + at % 3) for n, at in chunks for r in pair}
    operands = []

    def place(x):
        for i, y in enumerate(operands):
            if y is x:
                return i
        operands.append(x)
        return len(operands) - 1

    blocks = []
    edges = []
    for n in range(2):
        for conv in range(2):
            for s, (on_chip, off_chip, index, inner) in enumerate(halves[n][conv]):
                for r in range(1, rows + 1):
                    if (n, r) in needed:
                        x, before, at = inner[r - 1]
                        blocks.append(((n, conv, s, r), place(x), before, at))
                if (n, 0) in needed or (n, rows + 1) in needed:
                    edges.append(((n, conv, s), place(on_chip), place(off_chip), index))
    where = {key: rest for key, *rest in blocks}
    edge_at = {key: i for i, (key, *_) in enumerate(edges)}
    tables = [table for _, _, pair in jobs for table in pair]
    extra = [x for found in starts for _, x in found]
    offsets = [sum(len(found) for found in starts[:n]) for n in range(2)]
    count = len(halves[0][0])

    def body(core_ref, *refs):
        refs = list(refs)
        held = [refs.pop(0) for _ in operands]
        w_refs = [refs.pop(0) for _ in tables]
        s_refs = [refs.pop(0) for _ in extra]
        o_refs = [refs.pop(0) for _ in range(2)]
        if edges:
            low_ref, high_ref = refs.pop(0), refs.pop(0)

            @pl.when(core_ref[0] == 0)
            def _():
                for i, (_, on_chip, off_chip, index) in enumerate(edges):
                    high_ref[i] = held[on_chip][index]
                    low_ref[i] = held[off_chip][index]

            @pl.when(core_ref[0] != 0)
            def _():
                for i, (_, on_chip, off_chip, index) in enumerate(edges):
                    low_ref[i] = held[on_chip][index]
                    high_ref[i] = held[off_chip][index]

        if final:
            done_refs, sems = [refs.pop(0), refs.pop(0)], refs.pop(0)
        lane = lax.broadcasted_iota(jnp.int32, (outs, wide), 1) % cells
        first = lane == 0
        last = lane == cells - 1
        zero = jnp.zeros((count * part, cells), BF16)

        def source(n, conv, p, r):
            if p < 0 or p >= planes:
                return [zero]
            if r == 0:
                return [low_ref[edge_at[n, conv, s], p] for s in range(count)]
            if r == rows + 1:
                return [high_ref[edge_at[n, conv, s], p] for s in range(count)]
            found = []
            for s in range(count):
                operand, before, at = where[n, conv, s, r]
                found.append(held[operand][at, p] if before else held[operand][p, at])
            return found

        pending = []
        half = planes // 2
        for conv in range(2):
            for p in range(planes):
                for j, (pair, chunks, _) in enumerate(jobs):
                    columns = []
                    for r in pair:
                        stack = []
                        for n, at in chunks:
                            stack += source(n, conv, p + at // 3 - 1, r + at % 3)
                        columns.append(jnp.concatenate(stack, axis=0))
                    data = jnp.concatenate(columns, axis=1)
                    sums = jnp.dot(w_refs[2 * j + conv][...], data, preferred_element_type=jnp.float32)
                    total = sums[outs : 2 * outs]
                    total = total + jnp.where(first, 0.0, pltpu.roll(sums[:outs], 1, 1))
                    total = total + jnp.where(last, 0.0, pltpu.roll(sums[2 * outs :], wide - 1, 1))
                    for i, r in enumerate(pair):
                        piece = total[:, i * cells : (i + 1) * cells]
                        for m, (which, _) in enumerate(starts[conv]):
                            ref = s_refs[offsets[conv] + m]
                            if which is None:
                                piece = piece + ref[...]
                            elif r in which:
                                piece = piece + ref[p, which.index(r)]
                        if final:
                            done_refs[conv][p, r] = piece.astype(BF16)
                        else:
                            o_refs[conv][p, i] = piece
                if final and (p + 1) % half == 0:
                    span = pl.ds(p + 1 - half, half)
                    copy = pltpu.make_async_copy(
                        done_refs[conv].at[span], o_refs[conv].at[span], sems.at[len(pending)]
                    )
                    copy.start()
                    pending.append(copy)
        for copy in pending:
            copy.wait()

    kept = rows if final else 2
    out = jax.ShapeDtypeStruct((planes, kept, part, cells), BF16 if final else jnp.float32)
    scratch = []
    if edges:
        scratch += [pltpu.VMEM((len(edges), planes, part, cells), BF16)] * 2
    if final:
        scratch += [pltpu.VMEM(shape, BF16)] * 2 + [pltpu.SemaphoreType.DMA((4,))]
    depth = sum(len(chunks) for _, chunks, _ in jobs)
    return pl.pallas_call(
        body,
        out_shape=(out, out),
        in_specs=[SMEM, *[VMEM] * (len(operands) + len(tables) + len(extra))],
        out_specs=[pl.BlockSpec(memory_space=pl.ANY)] * 2 if final else [VMEM, VMEM],
        scratch_shapes=scratch,
        compiler_params=pltpu.CompilerParams(vmem_limit_bytes=14 * MIB),
        cost_estimate=pl.CostEstimate(
            flops=8 * 3 * outs * depth * count * part * planes * cells,
            bytes_accessed=6 * MIB,
            transcendentals=0,
        ),
    )(core, *operands, *tables, *extra)


def per_device(volume, kernel, bias, cotangent):
    size = lax.axis_size("chan")
    me = lax.axis_index("chan").astype(jnp.int32).reshape(1)
    core = (lax.axis_index("space") % 2).astype(jnp.int32).reshape(1)
    _, rows, _, _ = volume.shape

    vol_left = shifted(volume, 1)
    cot_right = shifted(cotangent, -1)
    own = jnp.swapaxes(kernel, 1, 2)
    vol_edge, cot_edge, on_chip, off_chip, wide, *sent = prologue(
        core, me, volume, cotangent, own, bias, size
    )
    received = [sent[0], *[shifted(sent[size - d], -d) for d in range(1, size)]]
    cot_left_edge = shifted(cot_edge, 1)
    vol_right_edge = shifted(vol_edge, -1)
    mine = swapped_rows(on_chip, off_chip)

    vol_edge, cot_edge, mid_up, mid_down = pack_forward(volume, cotangent, vol_left, cot_right)
    vol_edge, cot_edge = shifted(vol_edge, 1), shifted(cot_edge, -1)
    mid_up, mid_down = shifted(mid_up, 1), shifted(mid_down, -1)
    near = pack_rows(core, (vol_left, cot_right), (vol_right_edge, cot_left_edge))
    near = swapped_rows(*near)

    tables = weights(me, own, received, (INNER_ONE, OUTER_ONE, INNER_TWO, OUTER_TWO))
    inner_one, outer_one, inner_two, outer_two = (tables[n : n + 2] for n in range(0, 8, 2))

    far = pack_rows(core, (), (vol_edge, cot_edge))
    far = swapped_rows(*far)

    def whole(x, pair, n):
        return (*pair, n, [(x, False, r) for r in range(rows)])

    def split(edge, middle, half, pair, n):
        inner = [(middle, True, half * (rows - 2) + r) for r in range(rows - 2)]
        return (*pair, n, [(edge, True, 0), *inner, (edge, True, 1)])

    halves = (
        (
            [whole(vol_left, near, 0), whole(volume, mine, 0)],
            [whole(cotangent, mine, 1), whole(cot_right, near, 1)],
        ),
        (
            [split(vol_right_edge, mid_down, 0, near, 2), split(vol_edge, mid_up, 1, far, 0)],
            [split(cot_edge, mid_down, 1, far, 1), split(cot_left_edge, mid_up, 0, near, 3)],
        ),
    )
    inner, outer = tuple(range(1, rows - 1)), (0, rows - 1)
    starts = (((None, wide),), ())
    shape = volume.shape
    jobs = ((inner, INNER_ONE, inner_one),)
    insides = stage(core, halves, jobs, starts, shape, False)
    jobs = ((outer, OUTER_ONE, outer_one),)
    outsides = stage(core, halves, jobs, starts, shape, False)
    jobs = ((inner, INNER_TWO, inner_two), (outer, OUTER_TWO, outer_two))
    starts = tuple(((inner, insides[n]), (outer, outsides[n])) for n in range(2))
    return stage(core, halves, jobs, starts, shape, True)


def solution(mesh):
    spec = P(None, "space", "chan", None)

    return jax.shard_map(
        per_device,
        mesh=mesh,
        in_specs=(spec, P(None, None, "chan"), P("chan"), spec),
        out_specs=(spec, spec),
        check_vma=False,
    )
```

```python
import jax
import jax.numpy as jnp
from jax import lax
from jax.experimental import pallas as pl
from jax.experimental.pallas import tpu as pltpu
from jax.sharding import PartitionSpec as P


MIB = 1024 * 1024
BF16 = jnp.bfloat16
VMEM = pl.BlockSpec(memory_space=pltpu.VMEM)
SMEM = pl.BlockSpec(memory_space=pltpu.SMEM)


INNER_ONE = tuple((0, at) for at in range(8))
INNER_TWO = (*[(1, at) for at in range(9)], (0, 8))
OUTER_ONE = (*[(0, at) for at in range(9)], (1, 1), (1, 4), (1, 7))
OUTER_TWO = tuple((1, at) for at in (0, 2, 3, 5, 6, 8))


def shifted(x, steps):
    count = lax.axis_size("chan")
    return lax.ppermute(x, "chan", [(i, (i + steps) % count) for i in range(count)])


def swapped_rows(on_chip, off_chip):
    count = lax.axis_size("space")
    near = [(i, i ^ 1) for i in range(count)]
    far = [(i, i - 1 if i % 2 == 0 else i + 1) for i in range(1, count - 1)]
    off_chip = lax.ppermute(off_chip, "space", far)
    on_chip = lax.ppermute(on_chip, "space", near)
    return on_chip, off_chip


def pack_forward(volume, cotangent, vol_near, cot_near):
    planes, rows, part, cells = volume.shape
    inside = rows - 2

    def body(v, c, vn, cn, ev, ec, m_up, m_down):
        for x, edge in ((vn, ev), (cn, ec)):
            edge[0] = x[:, 0]
            edge[1] = x[:, rows - 1]
        for r in range(inside):
            for n, x in enumerate((c, vn)):
                m_up[n * inside + r] = x[:, 1 + r]
            for n, x in enumerate((v, cn)):
                m_down[n * inside + r] = x[:, 1 + r]

    def out(n):
        return jax.ShapeDtypeStruct((n, planes, part, cells), BF16)

    return pl.pallas_call(
        body,
        out_shape=(out(2), out(2), out(2 * inside), out(2 * inside)),
        in_specs=[VMEM] * 4,
        out_specs=[VMEM] * 4,
        compiler_params=pltpu.CompilerParams(vmem_limit_bytes=8 * MIB),
        name="pack_forward",
    )(volume, cotangent, vol_near, cot_near)


def pack_rows(core, wholes, edges, pieces=()):
    planes, part, cells = edges[0].shape[1:]
    count = len(wholes) + len(edges)
    more = 1 if pieces else 0

    def body(core_ref, *refs):
        *held, on_chip, off_chip = refs
        for n, x in enumerate(held[count:]):
            on_chip[count, pl.ds(n * x.shape[0], x.shape[0])] = x[...]
        held = held[:count]
        side = jnp.where(core_ref[0] == 0, 1, 0)
        for n, x in enumerate(held):
            if n < len(wholes):
                rows = x.shape[1]
                on_chip[n] = x[:, side * (rows - 1)]
                off_chip[n] = x[:, (1 - side) * (rows - 1)]
            else:
                on_chip[n] = x[side]
                off_chip[n] = x[1 - side]

    return pl.pallas_call(
        body,
        out_shape=tuple(
            jax.ShapeDtypeStruct((n, planes, part, cells), BF16) for n in (count + more, count)
        ),
        in_specs=[SMEM, *[VMEM] * (count + len(pieces))],
        out_specs=[VMEM] * 2,
        compiler_params=pltpu.CompilerParams(vmem_limit_bytes=8 * MIB),
    )(core, *wholes, *edges, *pieces)


def prologue(core, place, volume, cotangent, own, bias, size):
    planes, rows, part, cells = volume.shape
    taps, outs, chans = own.shape
    groups = -(-taps // (2 * size))

    def body(core_ref, place_ref, v, c, own_ref, bias_ref, *out_refs):
        ev, ec, on_chip, off_chip, wide_ref, *send_refs = out_refs
        side = jnp.where(core_ref[0] == 0, 1, 0)
        for n, (x, edge) in enumerate(((v, ev), (c, ec))):
            edge[0] = x[:, 0]
            edge[1] = x[:, rows - 1]
            on_chip[n] = x[:, side * (rows - 1)]
            off_chip[n] = x[:, (1 - side) * (rows - 1)]
        shape = (outs, outs)
        same = lax.broadcasted_iota(jnp.int32, shape, 0) == lax.broadcasted_iota(jnp.int32, shape, 1)
        column = jnp.sum(jnp.where(same, bias_ref[...], 0.0), axis=1, keepdims=True)
        wide_ref[...] = jnp.broadcast_to(column, wide_ref.shape)
        turn = lax.rem(size - place_ref[0], size) * part
        top = taps - 1 - core_ref[0] * (groups * size)
        for g in range(groups):
            quad = []
            for k in range(g * size, (g + 1) * size):
                tile = own_ref[jnp.maximum(top - k, 0)].astype(jnp.float32)
                quad.append(pltpu.roll(jnp.where(top >= k, tile, 0.0), turn, 1))
            for j in range(size):
                pieces = [q[:, j * part : (j + 1) * part] for q in quad]
                send_refs[j][g] = jnp.concatenate(pieces, axis=1).astype(BF16)

    two = jax.ShapeDtypeStruct((2, planes, part, cells), BF16)
    return pl.pallas_call(
        body,
        out_shape=(
            *[two] * 4,
            jax.ShapeDtypeStruct((outs, cells), jnp.float32),
            *[jax.ShapeDtypeStruct((groups, outs, chans), BF16)] * size,
        ),
        in_specs=[SMEM, SMEM, *[VMEM] * 4],
        out_specs=[VMEM] * (size + 5),
        compiler_params=pltpu.CompilerParams(vmem_limit_bytes=61 * MIB + MIB // 2),
        name="prologue",
    )(core, place, volume, cotangent, own, bias.reshape(1, outs))


def weights(core, place, own, received, others, layouts):
    taps, outs, chans = own.shape
    size, groups = len(received), received[0].shape[0]
    part = chans // size
    half = chans // 2

    last = others.shape[0] - 1

    def body(core_ref, place_ref, own_ref, others_ref, *refs):
        got_refs = refs[:size]
        table_refs = refs[size:]
        turn = lax.rem(size - place_ref[0] + 1, size) * part
        low = lax.broadcasted_iota(jnp.int32, (outs, chans), 1) < half

        def put(ref, chunks, tiles):
            for c in range(3):
                here = slice(c * outs, (c + 1) * outs)
                for k in range(0, len(chunks), 2):
                    found = []
                    for side, (n, at) in enumerate(chunks[k : k + 2]):
                        tile = tiles[3 * at + c]
                        found.append(tile if n == side else pltpu.roll(tile, half, 1))
                    if len(found) == 2:
                        both = jnp.where(low, *found)
                        ref[here, k * half : (k + 2) * half] = both.astype(BF16)
                    else:
                        ref[here, k * half :] = found[0][:, :half].astype(BF16)

        tiles = [pltpu.roll(own_ref[t].astype(jnp.float32), turn, 1) for t in range(taps)]
        for n, chunks in enumerate(layouts):
            put(table_refs[2 * n], chunks, tiles)
        tiles = []
        for g in range(2 * groups):
            at = g % groups
            mine = jnp.concatenate([got[at] for got in got_refs], axis=0).astype(jnp.float32)
            theirs = [others_ref[last, d * groups + at] for d in range(size)]
            theirs = jnp.concatenate(theirs, axis=0).astype(jnp.float32)
            tile = jnp.where(core_ref[0] == g // groups, mine, theirs).T
            tiles += [tile[t * part : (t + 1) * part] for t in range(size)]
        for n, chunks in enumerate(layouts):
            put(table_refs[2 * n + 1], chunks, tiles)

    shapes = [jax.ShapeDtypeStruct((3 * outs, len(chunks) * half), BF16) for chunks in layouts]
    return pl.pallas_call(
        body,
        out_shape=tuple(shape for shape in shapes for _ in range(2)),
        in_specs=[SMEM, SMEM, *[VMEM] * (size + 2)],
        out_specs=[VMEM] * (2 * len(layouts)),
        compiler_params=pltpu.CompilerParams(vmem_limit_bytes=8 * MIB),
        name="weights",
    )(core, place, own, others, *received)


def stage(core, halves, jobs, starts, shape, final):
    planes, rows, part, cells = shape
    outs = part
    wide = 2 * cells
    needed = set()
    for pair, chunks, _ in jobs:
        needed |= {(n, r + at % 3) for n, at in chunks for r in pair}
    operands = []

    def place(x):
        for i, y in enumerate(operands):
            if y is x:
                return i
        operands.append(x)
        return len(operands) - 1

    blocks = []
    edges = []
    for n in range(2):
        for conv in range(2):
            for s, (on_chip, off_chip, index, inner) in enumerate(halves[n][conv]):
                for r in range(1, rows + 1):
                    if (n, r) in needed:
                        x, before, at = inner[r - 1]
                        blocks.append(((n, conv, s, r), place(x), before, at))
                if (n, 0) in needed or (n, rows + 1) in needed:
                    edges.append(((n, conv, s), place(on_chip), place(off_chip), index))
    where = {key: rest for key, *rest in blocks}
    edge_at = {key: i for i, (key, *_) in enumerate(edges)}
    tables = [table for _, _, pair in jobs for table in pair]
    extra = [x for found in starts for _, x in found]
    offsets = [sum(len(found) for found in starts[:n]) for n in range(2)]
    count = len(halves[0][0])

    def body(core_ref, *refs):
        refs = list(refs)
        held = [refs.pop(0) for _ in operands]
        w_refs = [refs.pop(0) for _ in tables]
        s_refs = [refs.pop(0) for _ in extra]
        o_refs = [refs.pop(0) for _ in range(2)]
        if edges:
            low_ref, high_ref = refs.pop(0), refs.pop(0)

            @pl.when(core_ref[0] == 0)
            def _():
                for i, (_, on_chip, off_chip, index) in enumerate(edges):
                    high_ref[i] = held[on_chip][index]
                    low_ref[i] = held[off_chip][index]

            @pl.when(core_ref[0] != 0)
            def _():
                for i, (_, on_chip, off_chip, index) in enumerate(edges):
                    low_ref[i] = held[on_chip][index]
                    high_ref[i] = held[off_chip][index]

        if final:
            done_refs, sems = [refs.pop(0), refs.pop(0)], refs.pop(0)
        lane = lax.broadcasted_iota(jnp.int32, (outs, wide), 1) % cells
        first = lane == 0
        last = lane == cells - 1
        zero = jnp.zeros((count * part, cells), BF16)

        def source(n, conv, p, r):
            if p < 0 or p >= planes:
                return [zero]
            if r == 0:
                return [low_ref[edge_at[n, conv, s], p] for s in range(count)]
            if r == rows + 1:
                return [high_ref[edge_at[n, conv, s], p] for s in range(count)]
            found = []
            for s in range(count):
                operand, before, at = where[n, conv, s, r]
                found.append(held[operand][at, p] if before else held[operand][p, at])
            return found

        pending = []
        half = planes // 2
        for conv in range(2):
            for p in range(planes):
                for j, (pair, chunks, _) in enumerate(jobs):
                    columns = []
                    for r in pair:
                        stack = []
                        for n, at in chunks:
                            stack += source(n, conv, p + at // 3 - 1, r + at % 3)
                        columns.append(jnp.concatenate(stack, axis=0))
                    data = jnp.concatenate(columns, axis=1)
                    sums = jnp.dot(w_refs[2 * j + conv][...], data, preferred_element_type=jnp.float32)
                    total = sums[outs : 2 * outs]
                    total = total + jnp.where(first, 0.0, pltpu.roll(sums[:outs], 1, 1))
                    total = total + jnp.where(last, 0.0, pltpu.roll(sums[2 * outs :], wide - 1, 1))
                    for i, r in enumerate(pair):
                        piece = total[:, i * cells : (i + 1) * cells]
                        for m, (which, _) in enumerate(starts[conv]):
                            ref = s_refs[offsets[conv] + m]
                            if which is None:
                                piece = piece + ref[...]
                            elif r in which:
                                piece = piece + ref[p, which.index(r)]
                        if final:
                            done_refs[conv][p, r] = piece.astype(BF16)
                        else:
                            o_refs[conv][p, i] = piece
                if final and (p + 1) % half == 0:
                    span = pl.ds(p + 1 - half, half)
                    copy = pltpu.make_async_copy(
                        done_refs[conv].at[span], o_refs[conv].at[span], sems.at[len(pending)]
                    )
                    copy.start()
                    pending.append(copy)
        for copy in pending:
            copy.wait()

    kept = rows if final else 2
    out = jax.ShapeDtypeStruct((planes, kept, part, cells), BF16 if final else jnp.float32)
    scratch = []
    if edges:
        scratch += [pltpu.VMEM((len(edges), planes, part, cells), BF16)] * 2
    if final:
        scratch += [pltpu.VMEM(shape, BF16)] * 2 + [pltpu.SemaphoreType.DMA((4,))]
    depth = sum(len(chunks) for _, chunks, _ in jobs)
    return pl.pallas_call(
        body,
        out_shape=(out, out),
        in_specs=[SMEM, *[VMEM] * (len(operands) + len(tables) + len(extra))],
        out_specs=[pl.BlockSpec(memory_space=pl.ANY)] * 2 if final else [VMEM, VMEM],
        scratch_shapes=scratch,
        compiler_params=pltpu.CompilerParams(vmem_limit_bytes=14 * MIB),
        cost_estimate=pl.CostEstimate(
            flops=8 * 3 * outs * depth * count * part * planes * cells,
            bytes_accessed=6 * MIB,
            transcendentals=0,
        ),
    )(core, *operands, *tables, *extra)


def per_device(volume, kernel, bias, cotangent):
    size = lax.axis_size("chan")
    me = lax.axis_index("chan").astype(jnp.int32).reshape(1)
    core = (lax.axis_index("space") % 2).astype(jnp.int32).reshape(1)
    _, rows, _, _ = volume.shape

    vol_left = shifted(volume, 1)
    cot_right = shifted(cotangent, -1)
    own = jnp.swapaxes(kernel, 1, 2)
    vol_edge, cot_edge, on_chip, off_chip, wide, *sent = prologue(
        core, me, volume, cotangent, own, bias, size
    )
    received = [sent[0], *[shifted(sent[size - d], -d) for d in range(1, size)]]
    cot_left_edge = shifted(cot_edge, 1)
    vol_right_edge = shifted(vol_edge, -1)
    mine = swapped_rows(on_chip, off_chip)

    vol_edge, cot_edge, mid_up, mid_down = pack_forward(volume, cotangent, vol_left, cot_right)
    vol_edge, cot_edge = shifted(vol_edge, 1), shifted(cot_edge, -1)
    mid_up, mid_down = shifted(mid_up, 1), shifted(mid_down, -1)
    near = pack_rows(core, (vol_left, cot_right), (vol_right_edge, cot_left_edge), received)
    near = swapped_rows(*near)

    tables = weights(core, me, own, received, near[0], (INNER_ONE, OUTER_ONE, INNER_TWO, OUTER_TWO))
    inner_one, outer_one, inner_two, outer_two = (tables[n : n + 2] for n in range(0, 8, 2))

    far = pack_rows(core, (), (vol_edge, cot_edge))
    far = swapped_rows(*far)

    def whole(x, pair, n):
        return (*pair, n, [(x, False, r) for r in range(rows)])

    def split(edge, middle, half, pair, n):
        inner = [(middle, True, half * (rows - 2) + r) for r in range(rows - 2)]
        return (*pair, n, [(edge, True, 0), *inner, (edge, True, 1)])

    halves = (
        (
            [whole(vol_left, near, 0), whole(volume, mine, 0)],
            [whole(cotangent, mine, 1), whole(cot_right, near, 1)],
        ),
        (
            [split(vol_right_edge, mid_down, 0, near, 2), split(vol_edge, mid_up, 1, far, 0)],
            [split(cot_edge, mid_down, 1, far, 1), split(cot_left_edge, mid_up, 0, near, 3)],
        ),
    )
    inner, outer = tuple(range(1, rows - 1)), (0, rows - 1)
    starts = (((None, wide),), ())
    shape = volume.shape
    jobs = ((inner, INNER_ONE, inner_one),)
    insides = stage(core, halves, jobs, starts, shape, False)
    jobs = ((outer, OUTER_ONE, outer_one),)
    outsides = stage(core, halves, jobs, starts, shape, False)
    jobs = ((inner, INNER_TWO, inner_two), (outer, OUTER_TWO, outer_two))
    starts = tuple(((inner, insides[n]), (outer, outsides[n])) for n in range(2))
    return stage(core, halves, jobs, starts, shape, True)


def solution(mesh):
    spec = P(None, "space", "chan", None)

    return jax.shard_map(
        per_device,
        mesh=mesh,
        in_specs=(spec, P(None, None, "chan"), P("chan"), spec),
        out_specs=(spec, spec),
        check_vma=False,
    )
```

```python
import jax
import jax.numpy as jnp
from jax import lax
from jax.experimental import pallas as pl
from jax.experimental.pallas import tpu as pltpu
from jax.sharding import PartitionSpec as P


MIB = 1024 * 1024
BF16 = jnp.bfloat16
VMEM = pl.BlockSpec(memory_space=pltpu.VMEM)
SMEM = pl.BlockSpec(memory_space=pltpu.SMEM)


INNER_ONE = tuple((0, at) for at in range(8))
INNER_TWO = (*[(1, at) for at in range(9)], (0, 8))
OUTER_ONE = (*[(0, at) for at in range(9)], (1, 1), (1, 4), (1, 7))
OUTER_TWO = tuple((1, at) for at in (0, 2, 3, 5, 6, 8))
LAYOUTS = (INNER_ONE, OUTER_ONE, INNER_TWO, OUTER_TWO)


def shifted(x, steps):
    count = lax.axis_size("chan")
    return lax.ppermute(x, "chan", [(i, (i + steps) % count) for i in range(count)])


def swapped_rows(on_chip, off_chip):
    count = lax.axis_size("space")
    near = [(i, i ^ 1) for i in range(count)]
    far = [(i, i - 1 if i % 2 == 0 else i + 1) for i in range(1, count - 1)]
    off_chip = lax.ppermute(off_chip, "space", far)
    on_chip = lax.ppermute(on_chip, "space", near)
    return on_chip, off_chip


def pack_forward(volume, cotangent, vol_near, cot_near):
    planes, rows, part, cells = volume.shape
    inside = rows - 2

    def body(v, c, vn, cn, ev, ec, m_up, m_down):
        for x, edge in ((vn, ev), (cn, ec)):
            edge[0] = x[:, 0]
            edge[1] = x[:, rows - 1]
        for r in range(inside):
            for n, x in enumerate((c, vn)):
                m_up[n * inside + r] = x[:, 1 + r]
            for n, x in enumerate((v, cn)):
                m_down[n * inside + r] = x[:, 1 + r]

    def out(n):
        return jax.ShapeDtypeStruct((n, planes, part, cells), BF16)

    return pl.pallas_call(
        body,
        out_shape=(out(2), out(2), out(2 * inside), out(2 * inside)),
        in_specs=[VMEM] * 4,
        out_specs=[VMEM] * 4,
        compiler_params=pltpu.CompilerParams(vmem_limit_bytes=8 * MIB),
        name="pack_forward",
    )(volume, cotangent, vol_near, cot_near)


def pack_rows(core, wholes, edges, pieces=()):
    planes, part, cells = edges[0].shape[1:]
    count = len(wholes) + len(edges)
    more = 1 if pieces else 0

    def body(core_ref, *refs):
        *held, on_chip, off_chip = refs
        for n, x in enumerate(held[count:]):
            on_chip[count, pl.ds(n * x.shape[0], x.shape[0])] = x[...]
        held = held[:count]
        side = jnp.where(core_ref[0] == 0, 1, 0)
        for n, x in enumerate(held):
            if n < len(wholes):
                rows = x.shape[1]
                on_chip[n] = x[:, side * (rows - 1)]
                off_chip[n] = x[:, (1 - side) * (rows - 1)]
            else:
                on_chip[n] = x[side]
                off_chip[n] = x[1 - side]

    return pl.pallas_call(
        body,
        out_shape=tuple(
            jax.ShapeDtypeStruct((n, planes, part, cells), BF16) for n in (count + more, count)
        ),
        in_specs=[SMEM, *[VMEM] * (count + len(pieces))],
        out_specs=[VMEM] * 2,
        compiler_params=pltpu.CompilerParams(vmem_limit_bytes=8 * MIB),
    )(core, *wholes, *edges, *pieces)


def prologue(core, place, volume, cotangent, own, bias, size):
    planes, rows, part, cells = volume.shape
    taps, outs, chans = own.shape
    groups = -(-taps // (2 * size))

    def body(core_ref, place_ref, v, c, own_ref, bias_ref, *out_refs):
        ev, ec, on_chip, off_chip, wide_ref, *send_refs = out_refs
        side = jnp.where(core_ref[0] == 0, 1, 0)
        for n, (x, edge) in enumerate(((v, ev), (c, ec))):
            edge[0] = x[:, 0]
            edge[1] = x[:, rows - 1]
            on_chip[n] = x[:, side * (rows - 1)]
            off_chip[n] = x[:, (1 - side) * (rows - 1)]
        shape = (outs, outs)
        same = lax.broadcasted_iota(jnp.int32, shape, 0) == lax.broadcasted_iota(jnp.int32, shape, 1)
        column = jnp.sum(jnp.where(same, bias_ref[...], 0.0), axis=1, keepdims=True)
        wide_ref[...] = jnp.broadcast_to(column, wide_ref.shape)
        turn = lax.rem(size - place_ref[0], size) * part
        top = taps - 1 - core_ref[0] * (groups * size)
        for g in range(groups):
            quad = []
            for k in range(g * size, (g + 1) * size):
                tile = own_ref[jnp.maximum(top - k, 0)].astype(jnp.float32)
                quad.append(pltpu.roll(jnp.where(top >= k, tile, 0.0), turn, 1))
            for j in range(size):
                pieces = [q[:, j * part : (j + 1) * part] for q in quad]
                send_refs[j][g] = jnp.concatenate(pieces, axis=1).astype(BF16)

    two = jax.ShapeDtypeStruct((2, planes, part, cells), BF16)
    return pl.pallas_call(
        body,
        out_shape=(
            *[two] * 4,
            jax.ShapeDtypeStruct((outs, cells), jnp.float32),
            *[jax.ShapeDtypeStruct((groups, outs, chans), BF16)] * size,
        ),
        in_specs=[SMEM, SMEM, *[VMEM] * 4],
        out_specs=[VMEM] * (size + 5),
        compiler_params=pltpu.CompilerParams(vmem_limit_bytes=61 * MIB + MIB // 2),
        name="prologue",
    )(core, place, volume, cotangent, own, bias.reshape(1, outs))


def weights_back(core, received, others, layouts):
    size = len(received)
    groups, outs, chans = received[0].shape
    part = chans // size
    half = chans // 2

    last = others.shape[0] - 1

    def body(core_ref, others_ref, *refs):
        got_refs = refs[:size]
        table_refs = refs[size:]
        low = lax.broadcasted_iota(jnp.int32, (outs, chans), 1) < half

        def put(ref, chunks, tiles):
            for c in range(3):
                here = slice(c * outs, (c + 1) * outs)
                for k in range(0, len(chunks), 2):
                    found = []
                    for side, (n, at) in enumerate(chunks[k : k + 2]):
                        tile = tiles[3 * at + c]
                        found.append(tile if n == side else pltpu.roll(tile, half, 1))
                    if len(found) == 2:
                        both = jnp.where(low, *found)
                        ref[here, k * half : (k + 2) * half] = both.astype(BF16)
                    else:
                        ref[here, k * half :] = found[0][:, :half].astype(BF16)

        tiles = []
        for g in range(2 * groups):
            at = g % groups
            mine = jnp.concatenate([got[at] for got in got_refs], axis=0).astype(jnp.float32)
            theirs = [others_ref[last, d * groups + at] for d in range(size)]
            theirs = jnp.concatenate(theirs, axis=0).astype(jnp.float32)
            tile = jnp.where(core_ref[0] == g // groups, mine, theirs).T
            tiles += [tile[t * part : (t + 1) * part] for t in range(size)]
        for n, chunks in enumerate(layouts):
            put(table_refs[n], chunks, tiles)

    shapes = [jax.ShapeDtypeStruct((3 * outs, len(chunks) * half), BF16) for chunks in layouts]
    return pl.pallas_call(
        body,
        out_shape=tuple(shapes),
        in_specs=[SMEM, *[VMEM] * (size + 1)],
        out_specs=[VMEM] * len(layouts),
        compiler_params=pltpu.CompilerParams(vmem_limit_bytes=8 * MIB),
        name="weights_back",
    )(core, others, *received)


def weights_ahead(place, own, size, layouts):
    taps, outs, chans = own.shape
    part = chans // size
    half = chans // 2

    def body(place_ref, own_ref, *table_refs):
        turn = lax.rem(size - place_ref[0] + 1, size) * part
        low = lax.broadcasted_iota(jnp.int32, (outs, chans), 1) < half

        def put(ref, chunks, tiles):
            for c in range(3):
                here = slice(c * outs, (c + 1) * outs)
                for k in range(0, len(chunks), 2):
                    found = []
                    for side, (n, at) in enumerate(chunks[k : k + 2]):
                        tile = tiles[3 * at + c]
                        found.append(tile if n == side else pltpu.roll(tile, half, 1))
                    if len(found) == 2:
                        both = jnp.where(low, *found)
                        ref[here, k * half : (k + 2) * half] = both.astype(BF16)
                    else:
                        ref[here, k * half :] = found[0][:, :half].astype(BF16)

        tiles = [pltpu.roll(own_ref[t].astype(jnp.float32), turn, 1) for t in range(taps)]
        for n, chunks in enumerate(layouts):
            put(table_refs[n], chunks, tiles)

    return pl.pallas_call(
        body,
        out_shape=tuple(
            jax.ShapeDtypeStruct((3 * outs, len(chunks) * half), BF16) for chunks in layouts
        ),
        in_specs=[SMEM, VMEM],
        out_specs=[VMEM] * len(layouts),
        compiler_params=pltpu.CompilerParams(vmem_limit_bytes=8 * MIB),
        name="weights_ahead",
    )(place, own)


def stage(core, halves, jobs, starts, shape, final):
    planes, rows, part, cells = shape
    outs = part
    wide = 2 * cells
    needed = set()
    for pair, chunks, _ in jobs:
        needed |= {(n, r + at % 3) for n, at in chunks for r in pair}
    operands = []

    def place(x):
        for i, y in enumerate(operands):
            if y is x:
                return i
        operands.append(x)
        return len(operands) - 1

    blocks = []
    edges = []
    for n in range(2):
        for conv in range(2):
            for s, (on_chip, off_chip, index, inner) in enumerate(halves[n][conv]):
                for r in range(1, rows + 1):
                    if (n, r) in needed:
                        x, before, at = inner[r - 1]
                        blocks.append(((n, conv, s, r), place(x), before, at))
                if (n, 0) in needed or (n, rows + 1) in needed:
                    edges.append(((n, conv, s), place(on_chip), place(off_chip), index))
    where = {key: rest for key, *rest in blocks}
    edge_at = {key: i for i, (key, *_) in enumerate(edges)}
    tables = [table for _, _, pair in jobs for table in pair]
    extra = [x for found in starts for _, x in found]
    offsets = [sum(len(found) for found in starts[:n]) for n in range(2)]
    count = len(halves[0][0])

    def body(core_ref, *refs):
        refs = list(refs)
        held = [refs.pop(0) for _ in operands]
        w_refs = [refs.pop(0) for _ in tables]
        s_refs = [refs.pop(0) for _ in extra]
        o_refs = [refs.pop(0) for _ in range(2)]
        if edges:
            low_ref, high_ref = refs.pop(0), refs.pop(0)

            @pl.when(core_ref[0] == 0)
            def _():
                for i, (_, on_chip, off_chip, index) in enumerate(edges):
                    high_ref[i] = held[on_chip][index]
                    low_ref[i] = held[off_chip][index]

            @pl.when(core_ref[0] != 0)
            def _():
                for i, (_, on_chip, off_chip, index) in enumerate(edges):
                    low_ref[i] = held[on_chip][index]
                    high_ref[i] = held[off_chip][index]

        if final:
            done_refs, sems = [refs.pop(0), refs.pop(0)], refs.pop(0)
        lane = lax.broadcasted_iota(jnp.int32, (outs, wide), 1) % cells
        first = lane == 0
        last = lane == cells - 1
        zero = jnp.zeros((count * part, cells), BF16)

        def source(n, conv, p, r):
            if p < 0 or p >= planes:
                return [zero]
            if r == 0:
                return [low_ref[edge_at[n, conv, s], p] for s in range(count)]
            if r == rows + 1:
                return [high_ref[edge_at[n, conv, s], p] for s in range(count)]
            found = []
            for s in range(count):
                operand, before, at = where[n, conv, s, r]
                found.append(held[operand][at, p] if before else held[operand][p, at])
            return found

        pending = []
        half = planes // 2
        for conv in range(2):
            for p in range(planes):
                for j, (pair, chunks, _) in enumerate(jobs):
                    columns = []
                    for r in pair:
                        stack = []
                        for n, at in chunks:
                            stack += source(n, conv, p + at // 3 - 1, r + at % 3)
                        columns.append(jnp.concatenate(stack, axis=0))
                    data = jnp.concatenate(columns, axis=1)
                    sums = jnp.dot(w_refs[2 * j + conv][...], data, preferred_element_type=jnp.float32)
                    total = sums[outs : 2 * outs]
                    total = total + jnp.where(first, 0.0, pltpu.roll(sums[:outs], 1, 1))
                    total = total + jnp.where(last, 0.0, pltpu.roll(sums[2 * outs :], wide - 1, 1))
                    for i, r in enumerate(pair):
                        piece = total[:, i * cells : (i + 1) * cells]
                        for m, (which, _) in enumerate(starts[conv]):
                            ref = s_refs[offsets[conv] + m]
                            if which is None:
                                piece = piece + ref[...]
                            elif r in which:
                                piece = piece + ref[p, which.index(r)]
                        if final:
                            done_refs[conv][p, r] = piece.astype(BF16)
                        else:
                            o_refs[conv][p, i] = piece
                if final and (p + 1) % half == 0:
                    span = pl.ds(p + 1 - half, half)
                    copy = pltpu.make_async_copy(
                        done_refs[conv].at[span], o_refs[conv].at[span], sems.at[len(pending)]
                    )
                    copy.start()
                    pending.append(copy)
        for copy in pending:
            copy.wait()

    kept = rows if final else 2
    out = jax.ShapeDtypeStruct((planes, kept, part, cells), BF16 if final else jnp.float32)
    scratch = []
    if edges:
        scratch += [pltpu.VMEM((len(edges), planes, part, cells), BF16)] * 2
    if final:
        scratch += [pltpu.VMEM(shape, BF16)] * 2 + [pltpu.SemaphoreType.DMA((4,))]
    depth = sum(len(chunks) for _, chunks, _ in jobs)
    return pl.pallas_call(
        body,
        out_shape=(out, out),
        in_specs=[SMEM, *[VMEM] * (len(operands) + len(tables) + len(extra))],
        out_specs=[pl.BlockSpec(memory_space=pl.ANY)] * 2 if final else [VMEM, VMEM],
        scratch_shapes=scratch,
        compiler_params=pltpu.CompilerParams(vmem_limit_bytes=14 * MIB),
        cost_estimate=pl.CostEstimate(
            flops=8 * 3 * outs * depth * count * part * planes * cells,
            bytes_accessed=6 * MIB,
            transcendentals=0,
        ),
    )(core, *operands, *tables, *extra)


def per_device(volume, kernel, bias, cotangent):
    size = lax.axis_size("chan")
    me = lax.axis_index("chan").astype(jnp.int32).reshape(1)
    core = (lax.axis_index("space") % 2).astype(jnp.int32).reshape(1)
    _, rows, _, _ = volume.shape

    vol_left = shifted(volume, 1)
    cot_right = shifted(cotangent, -1)
    own = jnp.swapaxes(kernel, 1, 2)
    vol_edge, cot_edge, on_chip, off_chip, wide, *sent = prologue(
        core, me, volume, cotangent, own, bias, size
    )
    ahead = weights_ahead(me, own, size, LAYOUTS)
    received = [sent[0], *[shifted(sent[size - d], -d) for d in range(1, size)]]
    cot_left_edge = shifted(cot_edge, 1)
    vol_right_edge = shifted(vol_edge, -1)
    mine = swapped_rows(on_chip, off_chip)

    vol_edge, cot_edge, mid_up, mid_down = pack_forward(volume, cotangent, vol_left, cot_right)
    vol_edge, cot_edge = shifted(vol_edge, 1), shifted(cot_edge, -1)
    mid_up, mid_down = shifted(mid_up, 1), shifted(mid_down, -1)
    near = pack_rows(core, (vol_left, cot_right), (vol_right_edge, cot_left_edge), received)
    near = swapped_rows(*near)

    back = weights_back(core, received, near[0], LAYOUTS)
    inner_one, outer_one, inner_two, outer_two = zip(ahead, back)

    far = pack_rows(core, (), (vol_edge, cot_edge))
    far = swapped_rows(*far)

    def whole(x, pair, n):
        return (*pair, n, [(x, False, r) for r in range(rows)])

    def split(edge, middle, half, pair, n):
        inner = [(middle, True, half * (rows - 2) + r) for r in range(rows - 2)]
        return (*pair, n, [(edge, True, 0), *inner, (edge, True, 1)])

    halves = (
        (
            [whole(vol_left, near, 0), whole(volume, mine, 0)],
            [whole(cotangent, mine, 1), whole(cot_right, near, 1)],
        ),
        (
            [split(vol_right_edge, mid_down, 0, near, 2), split(vol_edge, mid_up, 1, far, 0)],
            [split(cot_edge, mid_down, 1, far, 1), split(cot_left_edge, mid_up, 0, near, 3)],
        ),
    )
    inner, outer = tuple(range(1, rows - 1)), (0, rows - 1)
    starts = (((None, wide),), ())
    shape = volume.shape
    jobs = ((inner, INNER_ONE, inner_one),)
    insides = stage(core, halves, jobs, starts, shape, False)
    jobs = ((outer, OUTER_ONE, outer_one),)
    outsides = stage(core, halves, jobs, starts, shape, False)
    jobs = ((inner, INNER_TWO, inner_two), (outer, OUTER_TWO, outer_two))
    starts = tuple(((inner, insides[n]), (outer, outsides[n])) for n in range(2))
    return stage(core, halves, jobs, starts, shape, True)


def solution(mesh):
    spec = P(None, "space", "chan", None)

    return jax.shard_map(
        per_device,
        mesh=mesh,
        in_specs=(spec, P(None, None, "chan"), P("chan"), spec),
        out_specs=(spec, spec),
        check_vma=False,
    )
```
